32 devices in a mesh: member: 4 (over y, x), lat: 8 (over z, core).
Axes of the slice: x: 2, y: 2, z: 4, core: 2. Of those that a mesh axis runs over, the one named last changes fastest.
Arguments:
- ensemble_starting_fields: bfloat16 [4, 256, 512, 384], P('member', 'lat'), may hold values from -6 to 6
- observed: bfloat16 [256, 512, 384], P('lat'), may hold values from -6 to 6
- wave_of_slot: int32 [256], replicated, may hold values from 0 to 255, each once
- leg_forward: bfloat16 [256, 256, 256], P('lat'), may hold values from -0.375 to 0.375
- leg_inverse: bfloat16 [256, 256, 256], P('lat'), may hold values from -0.375 to 0.375
- spec_filter: float32 [2, 256, 384], replicated, may hold values from -5 to 5
- gain_first: float32 [384], replicated, may hold values from 0.5 to 1.5
- gain_second: float32 [384], replicated, may hold values from 0.5 to 1.5
- weight_in: bfloat16 [384, 768], replicated, may hold values from -0.3125 to 0.3125
- weight_out: bfloat16 [768, 384], replicated, may hold values from -0.21875 to 0.21875
Outputs:
- predicted_field: bfloat16 [4, 256, 512, 384], P('member', 'lat')
- proper_loss_slope: bfloat16 [4, 256, 512, 384], P('member', 'lat')
The draws below stay inside these ranges and needn't reach their ends.
Inputs may be any that keep to these rules, and one draw needn't show every extreme that they name: `wave_of_slot`: every wavenumber 0 to 255 sits in exactly one slot.
All inputs are finite; a program needn't handle non-finite values.
Results may differ from the reference program's by a relative error of at most 0.013.
Values may be sent and summed in bfloat16 or wider, within the bound.
No kernel may reach another device: no remote copies, remote signals or barrier semaphores. Data moves between devices by JAX's collectives and lax.ppermute only.
A program may use at most 192 MiB of HBM per device.

```python
import jax
import jax.numpy as jnp
from jax import lax

NLAT = 256
NLON = 512
L = 256
M = 256
C = 384
FFN = 768
MEMBERS = 4


def shard_levels(rng, shape, shards, least, high):
    level = 1.0
    for dim, shards_of in shards:
        draws = jax.random.uniform(jax.random.fold_in(jax.random.fold_in(rng, 6), dim), (shards_of,), jnp.float32, least / len(shards), high / len(shards))
        level = level * jnp.repeat(jnp.exp(draws), shape[dim] // shards_of).reshape((-1,) + (1,) * (len(shape) - 1 - dim))
    return level


def scatter_about(key, shape, scale, bound, pieces=(), kind=jnp.bfloat16):
    drawn = scale * jax.random.normal(key, shape, jnp.float32)
    if pieces:
        drawn = drawn * shard_levels(key, shape, pieces, -0.22, 0.18)
    return jnp.clip(drawn, -bound, bound).astype(kind)


def setup_inputs(seed: int = 0) -> dict:
    key_list = jax.random.split(jax.random.key(seed), 11)
    return {
        "ensemble_starting_fields": scatter_about(key_list[0], (MEMBERS, NLAT, NLON, C), 1.0, 6.0, ((0, 4), (1, 8))),
        "observed": scatter_about(key_list[1], (NLAT, NLON, C), 1.0, 6.0, ((0, 8),)),
        "wave_of_slot": jax.random.permutation(key_list[2], M).astype(jnp.int32),
        "leg_forward": scatter_about(key_list[3], (M, L, NLAT), NLAT ** -0.5, 0.375, ((0, 8),)),
        "leg_inverse": scatter_about(key_list[4], (M, NLAT, L), L ** -0.5, 0.375, ((0, 8),)),
        "spec_filter": scatter_about(key_list[5], (2, L, C), 1.0, 5.0, (), jnp.float32),
        "gain_first": jnp.clip(1.0 + 0.1 * jax.random.normal(key_list[6], (C,), jnp.float32), 0.5, 1.5),
        "gain_second": jnp.clip(1.0 + 0.1 * jax.random.normal(key_list[7], (C,), jnp.float32), 0.5, 1.5),
        "weight_in": scatter_about(key_list[8], (C, FFN), C ** -0.5, 0.3125),
        "weight_out": scatter_about(key_list[9], (FFN, C), FFN ** -0.5, 0.21875),
    }


EPS_NORM = 1e-05
EPS_DIST = 1e-06

def layer_norm(values, scales):
    average = lax.optimization_barrier(jnp.mean(values, -1, keepdims=True))
    centred = values - average
    spread = lax.optimization_barrier(jnp.mean(centred * centred, -1, keepdims=True))
    return centred * lax.rsqrt(spread + EPS_NORM) * scales

def distance(first, second):
    return jnp.sqrt(lax.optimization_barrier(jnp.mean(jnp.square(first - second), -1, keepdims=True)) + EPS_DIST)

def reference(ensemble_starting_fields, observed, wave_of_slot, leg_forward, leg_inverse, spec_filter, gain_first, gain_second, weight_in, weight_out):
    order = jnp.arange(L, dtype=jnp.int32)
    retain = (order[None, :] >= wave_of_slot[:, None]).astype(jnp.float32)[:, None, :, None]
    nonzero = (wave_of_slot != 0).astype(jnp.float32)
    table_fwd = leg_forward.astype(jnp.float32)
    table_inv = leg_inverse.astype(jnp.float32)

    def ensemble_increment(state):
        values = state.astype(jnp.float32)
        normed = layer_norm(values, gain_first).astype(jnp.bfloat16)
        spectrum = jnp.fft.rfft(normed.astype(jnp.float32), axis=1) / NLON
        picked = spectrum[:, wave_of_slot, :]
        analysis = jnp.stack([jnp.real(picked), jnp.imag(picked)], 0).astype(jnp.bfloat16)
        coeffs = jnp.einsum('sln,rnsc->srlc', table_fwd, analysis.astype(jnp.float32)) * retain
        real_part = coeffs[:, 0]
        imag_part = coeffs[:, 1]
        filt_real = spec_filter[0]
        filt_imag = spec_filter[1]
        filtered = jnp.stack([real_part * filt_real - imag_part * filt_imag, real_part * filt_imag + imag_part * filt_real], 1).astype(jnp.bfloat16)
        synthesis = jnp.einsum('snl,srlc->srnc', table_inv, filtered.astype(jnp.float32)).astype(jnp.bfloat16)
        synth_real = jnp.transpose(synthesis[:, 0].astype(jnp.float32), (1, 0, 2))
        synth_imag = jnp.transpose(synthesis[:, 1].astype(jnp.float32), (1, 0, 2)) * nonzero[None, :, None]
        blank = jnp.zeros((NLAT, NLON // 2 + 1, C), jnp.float32)
        spectra_full = lax.complex(blank, blank)
        spectra_full = spectra_full.at[:, wave_of_slot, :].set(lax.complex(synth_real, synth_imag))
        spectral = jnp.fft.irfft(spectra_full, n=NLON, axis=1) * NLON
        harmonic_damped_field = values + spectral
        normed_two = layer_norm(harmonic_damped_field, gain_second).astype(jnp.bfloat16).reshape(NLAT * NLON, C)
        hidden = jax.nn.gelu(jnp.dot(normed_two.astype(jnp.float32), weight_in.astype(jnp.float32), preferred_element_type=jnp.float32)).astype(jnp.bfloat16)
        feedforward_result = jnp.dot(hidden.astype(jnp.float32), weight_out.astype(jnp.float32), preferred_element_type=jnp.float32)
        return (harmonic_damped_field + feedforward_result.reshape(NLAT, NLON, C)).astype(jnp.bfloat16)
    predicted_field = lax.map(ensemble_increment, ensemble_starting_fields)

    def score_row(operands):
        rows, target_row = operands
        ensemble = rows.astype(jnp.float32)
        target = target_row.astype(jnp.float32)
        members = ensemble.shape[0]
        grads = []
        for member_index in range(members):
            own = ensemble[member_index]
            pulled = jnp.zeros_like(own)
            for other in range(members):
                pulled = pulled + (own - ensemble[other]) / distance(own, ensemble[other])
            grads.append((own - target) / distance(own, target) - pulled / (members - 1))
        return jnp.stack(grads, 0).astype(jnp.bfloat16)
    latitude_bands = jnp.moveaxis(predicted_field, 1, 0)
    score_rows = lax.map(score_row, (latitude_bands, observed))
    proper_loss_slope = jnp.moveaxis(score_rows, 0, 1)
    return (predicted_field, proper_loss_slope)
```

```python
import functools
import math

import jax
import jax.numpy as jnp
from jax import lax
from jax.experimental import pallas as pl
from jax.experimental.pallas import tpu as pltpu
from jax.sharding import PartitionSpec as P


EPS_NORM = 1e-05
EPS_DIST = 1e-06
LANES = 128
BAND = 8
PART = 64
FINE = 16
SPAN = 256
EARLY = 2
NUMBER = 8
F32 = jnp.float32
BF16 = jnp.bfloat16


def layer_norm(values, scales):
    average = jnp.mean(values, -1, keepdims=True)
    centred = values - average
    spread = jnp.mean(centred * centred, -1, keepdims=True)
    return centred * lax.rsqrt(spread + EPS_NORM) * scales


def matmul(left, right):
    return jnp.dot(left, right, preferred_element_type=F32)


def params(**extra):
    return pltpu.CompilerParams(vmem_limit_bytes=56 << 20, **extra)


def cost(flops, bytes_accessed):
    return pl.CostEstimate(flops=int(flops), bytes_accessed=int(bytes_accessed), transcendentals=0)


def anywhere():
    return pl.BlockSpec(memory_space=pl.ANY)


def analysis_body(parts, field_ref, gain_ref, table_ref, *refs):
    outs = refs[:parts]
    normed, held = refs[parts:]
    band, length, channels = field_ref.shape
    orders = table_ref.shape[0]
    each = orders // parts
    pair = normed.shape[0]

    def some_rows(step, carry):
        for lane in range(pair):
            row = step * pair + lane
            for start in range(0, length, PART):
                values = field_ref[row, start : start + PART, :].astype(F32)
                normed[lane, start : start + PART, :] = layer_norm(values, gain_ref[...]).astype(
                    BF16
                )
            lines = matmul(table_ref[...], normed[lane])
            for tile in range(channels // LANES):
                held[tile, pl.ds(pl.multiple_of(row * orders, orders), orders), :] = lines[
                    :, tile * LANES : (tile + 1) * LANES
                ]
        return carry

    lax.fori_loop(0, band // pair, some_rows, 0)
    for part in range(parts):

        def one_order(index, carry, part=part):
            for tile in range(channels // LANES):
                outs[part][index, :, tile * LANES : (tile + 1) * LANES] = held[
                    tile, pl.ds(part * each + index, band, stride=orders), :
                ].astype(BF16)
            return carry

        lax.fori_loop(0, each, one_order, 0, unroll=8)


def analyse(field, gain, table, parts, first, count):
    _, length, channels = field.shape
    orders = table.shape[0]
    each = orders // parts
    return pl.pallas_call(
        functools.partial(analysis_body, parts),
        grid=(count // BAND,),
        in_specs=[
            pl.BlockSpec((BAND, length, channels), lambda i: (first // BAND + i, 0, 0)),
            pl.BlockSpec((1, channels), lambda i: (0, 0)),
            pl.BlockSpec((orders, length), lambda i: (0, 0)),
        ],
        out_specs=[pl.BlockSpec((each, BAND, channels), lambda i: (0, i, 0))] * parts,
        out_shape=[jax.ShapeDtypeStruct((each, count, channels), BF16)] * parts,
        scratch_shapes=[
            pltpu.VMEM((2, length, channels), BF16),
            pltpu.VMEM((channels // LANES, BAND * orders, LANES), F32),
        ],
        compiler_params=params(),
        cost_estimate=cost(2 * count * orders * length * channels, 3 * count * length * channels),
    )(field, gain, table)


def spectral_body(parts, total, offsets, targets, passed, scalars, *refs):
    pieces = len(offsets)
    slabs = refs[: pieces * parts]
    forward_ref, inverse_ref, filter_ref = refs[pieces * parts : pieces * parts + 3]
    first = pieces * parts + 3 + passed
    count = len(targets) * parts
    outs = refs[first : first + count]
    spectra, held = refs[first + count :]
    slot = pl.program_id(0)
    own = scalars[0]
    wave = scalars[2 + slot]
    degrees, latitudes = forward_ref.shape[1:]
    channels = filter_ref.shape[2]
    for piece in range(pieces):
        for part in range(parts):
            slab = slabs[piece * parts + part]
            rows = slab.shape[1]
            origin = lax.rem(own + parts - part, parts) * total + offsets[piece]
            place = pl.ds(pl.multiple_of(origin, rows), rows)
            for ri in range(2):
                spectra[ri, place, :] = slab[ri]
    order = lax.broadcasted_iota(jnp.int32, (degrees, 1), 0)
    retain = order >= wave
    for tile in range(channels // LANES):
        lanes = slice(tile * LANES, (tile + 1) * LANES)
        both = jnp.concatenate([spectra[0, :, lanes], spectra[1, :, lanes]], 1)
        coeffs = matmul(forward_ref[0], both)
        coeffs = jnp.where(retain, coeffs, 0.0)
        real_part, imag_part = coeffs[:, :LANES], coeffs[:, LANES:]
        filt_real, filt_imag = filter_ref[0, :, lanes], filter_ref[1, :, lanes]
        filtered = jnp.concatenate(
            [
                (real_part * filt_real - imag_part * filt_imag).astype(BF16),
                (real_part * filt_imag + imag_part * filt_real).astype(BF16),
            ],
            1,
        )
        profile = matmul(inverse_ref[0], filtered)
        for ri in range(2):
            start = pl.multiple_of((2 * slot + ri) * latitudes, latitudes)
            held[tile, pl.ds(start, latitudes), :] = profile[:, ri * LANES : (ri + 1) * LANES]

    @pl.when(slot == pl.num_programs(0) - 1)
    def _():
        for index, (offset, size) in enumerate(targets):
            for part in range(parts):
                out = outs[index * parts + part]
                base = lax.rem(own + part, parts) * total + offset

                def one_row(row, carry, out=out, base=base):
                    for tile in range(channels // LANES):
                        out[row, :, tile * LANES : (tile + 1) * LANES] = held[
                            tile, pl.ds(base + row, out.shape[1], stride=latitudes), :
                        ].astype(BF16)
                    return carry

                lax.fori_loop(0, size, one_row, 0, unroll=4)


def spectral(scalars, pieces, forward, inverse, spec_filter, first, number, targets):
    parts = len(pieces[0][1])
    degrees, latitudes = forward.shape[1:]
    channels = spec_filter.shape[2]
    operands = []
    in_specs = []
    for _, slabs in pieces:
        for slab in slabs:
            operands.append(slab)
            in_specs.append(pl.BlockSpec((2,) + slab.shape[1:], lambda s, *_: (s, 0, 0)))
    operands += [forward, inverse, spec_filter]
    in_specs += [
        pl.BlockSpec((1, degrees, latitudes), lambda s, *_: (first + s, 0, 0)),
        pl.BlockSpec((1, latitudes, degrees), lambda s, *_: (first + s, 0, 0)),
        pl.BlockSpec((2, degrees, channels), lambda s, *_: (0, 0, 0)),
    ]
    out_shape = []
    out_specs = []
    aliases = {}
    passed = 0
    for _, size, held_slots, block, carried in targets:
        for part in range(parts):
            if carried is not None:
                aliases[1 + len(operands)] = len(out_shape)
                operands.append(carried[part])
                in_specs.append(anywhere())
                passed += 1
            out_shape.append(jax.ShapeDtypeStruct((size, 2 * held_slots, channels), BF16))
            out_specs.append(
                pl.BlockSpec((size, 2 * number, channels), lambda s, *_, block=block: (0, block, 0))
            )
    outs = pl.pallas_call(
        functools.partial(
            spectral_body,
            parts,
            latitudes // parts,
            tuple(offset for offset, _ in pieces),
            tuple(target[:2] for target in targets),
            passed,
        ),
        grid_spec=pltpu.PrefetchScalarGridSpec(
            num_scalar_prefetch=1,
            grid=(number,),
            in_specs=in_specs,
            out_specs=out_specs,
            scratch_shapes=[
                pltpu.VMEM((2, latitudes, channels), BF16),
                pltpu.VMEM((channels // LANES, 2 * number * latitudes, LANES), F32),
            ],
        ),
        out_shape=out_shape,
        input_output_aliases=aliases,
        compiler_params=params(),
        cost_estimate=cost(
            8 * number * degrees * latitudes * channels,
            8 * number * latitudes * channels + 4 * number * degrees * latitudes,
        ),
    )(scalars, *operands)
    return [outs[index * parts : (index + 1) * parts] for index in range(len(targets))]


def finish_body(parts, members, continued, scalars, *refs):
    slabs = refs[:parts]
    field_ref, table_ref, gain_ref, into_ref, from_ref = refs[parts : parts + 5]
    first = parts + 5 + (1 if continued else 0)
    predicted_ref = refs[first]
    sends = refs[first + 1 : first + 1 + members]
    after_ref, normed_ref = refs[first + 1 + members :]
    length = field_ref.shape[1]
    lines = jnp.concatenate([slab[0] for slab in slabs], 0)
    after_ref[...] = matmul(table_ref[...], lines) + field_ref[0].astype(F32)
    for start in range(0, length, PART):
        normed_ref[start : start + PART, :] = layer_norm(
            after_ref[start : start + PART, :], gain_ref[...]
        ).astype(BF16)
    step = 256 if length % 256 == 0 else length
    for start in range(0, length, step):
        rows = slice(start, start + step)
        hidden = jax.nn.gelu(matmul(normed_ref[rows, :], into_ref[...])).astype(BF16)
        predicted_ref[0, rows, :] = (after_ref[rows, :] + matmul(hidden, from_ref[...])).astype(
            BF16
        )
    share = pl.num_programs(0) // members
    for part in range(members):

        @pl.when(pl.program_id(0) // share == part)
        def _(part=part):
            sends[part][0] = predicted_ref[0]


def finish(scalars, slabs, field, table, gain, into, out_of, carried, offset, members):
    parts = len(slabs)
    size, _, channels = slabs[0].shape
    _, length = field.shape[:2]
    share = size // members

    def position(r, sc):
        return lax.rem(sc[1] + r // share, members) * share + lax.rem(r, share)

    def whole(r, sc):
        return (offset + position(r, sc), 0, 0)

    def fixed(r, sc):
        return (0, 0)

    in_specs = [
        pl.BlockSpec((1,) + slab.shape[1:], lambda r, sc: (position(r, sc), 0, 0))
        for slab in slabs
    ]
    in_specs += [
        pl.BlockSpec((1, length, channels), whole),
        pl.BlockSpec(table.shape, fixed),
        pl.BlockSpec(gain.shape, fixed),
        pl.BlockSpec(into.shape, fixed),
        pl.BlockSpec(out_of.shape, fixed),
    ]
    aliases = {}
    if carried is not None:
        in_specs.append(anywhere())
        aliases = {1 + parts + 5: 0}
    out_specs = [pl.BlockSpec((1, length, channels), whole)]
    out_shape = [jax.ShapeDtypeStruct(field.shape, BF16)]
    for part in range(members):
        out_specs.append(
            pl.BlockSpec(
                (1, length, channels),
                lambda r, sc, part=part: (jnp.clip(r - part * share, 0, share - 1), 0, 0),
            )
        )
        out_shape.append(jax.ShapeDtypeStruct((share, length, channels), BF16))
    hidden = into.shape[1]
    return pl.pallas_call(
        functools.partial(finish_body, parts, members, carried is not None),
        grid_spec=pltpu.PrefetchScalarGridSpec(
            num_scalar_prefetch=1,
            grid=(size,),
            in_specs=in_specs,
            out_specs=out_specs,
            scratch_shapes=[
                pltpu.VMEM((length, channels), F32),
                pltpu.VMEM((length, channels), BF16),
            ],
        ),
        out_shape=out_shape,
        input_output_aliases=aliases,
        compiler_params=params(),
        cost_estimate=cost(
            2 * size * length * channels * (table.shape[1] + 2 * hidden),
            8 * size * length * channels,
        ),
    )(scalars, *slabs, field, table, gain, into, out_of, *([] if carried is None else [carried]))


def score_body(members, continued, scalars, *refs):
    fields = refs[:members]
    target_ref = refs[members]
    outs = refs[members + 1 + continued :]
    length, channels = target_ref.shape[1:]

    def one_part(index, carry):
        place = pl.ds(pl.multiple_of(index * FINE, FINE), FINE)
        values = [field[0, place, :].astype(F32) for field in fields]
        target = target_ref[0, place, :].astype(F32)

        def pull(first, second, scale):
            apart = first - second
            mean_square = jnp.sum(apart * apart, -1, keepdims=True) * (1.0 / channels)
            return apart * (lax.rsqrt(mean_square + EPS_DIST) * scale)

        slopes = [pull(value, target, 1.0) for value in values]
        for one in range(members):
            for other in range(one + 1, members):
                term = pull(values[one], values[other], 1.0 / (members - 1))
                slopes[one] = slopes[one] - term
                slopes[other] = slopes[other] + term
        for one in range(members):
            outs[one][0, place, :] = slopes[one].astype(BF16)
        return carry

    lax.fori_loop(0, length // FINE, one_part, 0, unroll=2)


def score(scalars, fields, observed, carried, offset):
    members = len(fields)
    share, length, channels = fields[0].shape

    def block(r, j, sc):
        return (r, j, 0)

    def whole(r, j, sc):
        return (offset + sc[1] * share + r, j, 0)

    span = SPAN if length % SPAN == 0 else length
    spec = pl.BlockSpec((1, span, channels), block)
    placed = pl.BlockSpec((1, span, channels), whole)
    piece = jax.ShapeDtypeStruct((share, length, channels), BF16)
    out_specs = [placed] + [spec] * (members - 1)
    out_shape = [jax.ShapeDtypeStruct(observed.shape, BF16)] + [piece] * (members - 1)
    continued = carried is not None
    return pl.pallas_call(
        functools.partial(score_body, members, continued),
        grid_spec=pltpu.PrefetchScalarGridSpec(
            num_scalar_prefetch=1,
            grid=(share, length // span),
            in_specs=[spec] * members + [placed] + [anywhere()] * continued,
            out_specs=out_specs,
        ),
        out_shape=out_shape,
        input_output_aliases={members + 2: 0} if continued else {},
        compiler_params=params(),
        cost_estimate=cost(100 * share * length * channels, 18 * share * length * channels),
    )(scalars, *fields, observed, *([carried] if continued else []))


def shift(array, axis, step):
    size = lax.axis_size(axis)
    return lax.ppermute(array, axis, [(i, (i + step) % size) for i in range(size)])


def place(whole, pieces):
    for piece, start in pieces:
        whole = lax.dynamic_update_slice_in_dim(whole, piece, start, 0)
    return whole


def angles_of(numbers, columns, length):
    phases = numbers * columns % length
    return phases.astype(F32) * (2.0 * math.pi / length)


def chunk_sizes(rows, unit):
    units = rows // unit
    if units < 6:
        return (unit,) * units
    middle = units - 4
    sizes = [1, 1] + [2] * (middle // 2) + [1] * (middle % 2) + [1, 1]
    return tuple(unit * size for size in sizes)


def pipelined(
    field,
    observed,
    wave_of_slot,
    leg_forward,
    leg_inverse,
    spec_filter,
    gain_first,
    gain_second,
    weight_in,
    weight_out,
):
    rows, length, channels = field.shape
    slots = leg_forward.shape[0]
    parts = lax.axis_size("lat")
    members = lax.axis_size("member")
    own = lax.axis_index("lat")
    own_member = lax.axis_index("member")
    number = NUMBER
    groups = slots // number
    chunks = chunk_sizes(rows, members)
    gain_first = gain_first.reshape(1, channels)
    gain_second = gain_second.reshape(1, channels)
    scalars = jnp.stack([own, own_member]).astype(jnp.int32)

    waves = wave_of_slot.reshape(parts, groups, number)
    steps = jnp.arange(parts, dtype=jnp.int32)
    columns = jnp.arange(length, dtype=jnp.int32)
    outgoing = jnp.take(waves, (own + steps) % parts, axis=0).transpose(1, 0, 2)
    angles = angles_of(outgoing[..., None, None], columns, length)
    turn = jnp.arange(2, dtype=jnp.int32)[:, None]
    tables = jnp.where(turn == 0, jnp.cos(angles), -jnp.sin(angles)) * (1.0 / length)
    tables = tables.astype(BF16).reshape(groups, parts * number * 2, length)
    incoming = jnp.take(wave_of_slot.reshape(parts, slots), (own - steps) % parts, axis=0)
    incoming = jnp.repeat(incoming.reshape(-1), 2)
    angles = angles_of(incoming[None, :], columns[:, None], length)
    weights = jnp.where(incoming == 0, 1.0, 2.0).astype(F32)[None, :]
    even = (jnp.arange(incoming.shape[0]) % 2 == 0)[None, :]
    back_table = (weights * jnp.where(even, jnp.cos(angles), -jnp.sin(angles))).astype(BF16)
    local_waves = lax.dynamic_slice_in_dim(wave_of_slot, own * slots, slots)

    def spread(slabs):
        return [slabs[0]] + [shift(slabs[part], "lat", part) for part in range(1, parts)]

    received = []
    for group in range(groups):
        halves = 2 if group == 0 else 1
        pieces = []
        for half in range(halves):
            count = rows // halves
            slabs = analyse(field, gain_first, tables[group], parts, half * count, count)
            pieces.append((half * count, spread(slabs)))
        received.append(pieces)
    starts = [sum(chunks[:index]) for index in range(len(chunks))]
    early = [None] * EARLY
    profiles = [None] * len(chunks)
    for group in range(groups):
        numbers = jnp.concatenate(
            [scalars, local_waves[group * number : (group + 1) * number]]
        )
        last = group == groups - 1
        targets = []
        for index in range(len(chunks)):
            place_of = (starts[index], chunks[index])
            if index >= EARLY:
                targets.append(place_of + (slots, group, profiles[index]))
            elif last:
                targets.append(place_of + (number, 0, None))
            else:
                targets.append(place_of + (slots - number, group, early[index]))
        profiles = spectral(
            numbers,
            received[group],
            leg_forward,
            leg_inverse,
            spec_filter,
            group * number,
            number,
            targets,
        )
        if not last:
            early = profiles[:EARLY]
        if group == groups - 2:
            arrived = []
            for index in range(EARLY):
                arrived.append(spread(early[index]))

    predicted = None
    slope = None
    offset = 0
    placed = []
    for index, size in enumerate(chunks):
        slabs = spread(profiles[index])
        if index < EARLY:
            slabs = [slab for both in zip(arrived[index], slabs) for slab in both]
        predicted, *sends = finish(
            scalars,
            slabs,
            field,
            back_table,
            gain_second,
            weight_in,
            weight_out,
            predicted,
            offset,
            members,
        )
        fields = [sends[0]] + [
            shift(sends[part], "member", part) for part in range(1, members)
        ]
        slope, *grads = score(scalars, fields, observed, slope, offset)
        share = size // members
        pieces = []
        for part in range(1, members):
            back = shift(grads[part - 1], "member", members - part)
            pieces.append((back, offset + (own_member + part) % members * share))
        placed.append(pieces)
        offset += size
        if index >= 2:
            slope = place(slope, placed[index - 2])
    for pieces in placed[max(len(chunks) - 2, 0) :]:
        slope = place(slope, pieces)
    return predicted[None], slope[None]


def distance(first, second):
    return jnp.sqrt(jnp.mean(jnp.square(first - second), -1, keepdims=True) + EPS_DIST)


def dft_tables(numbers, length):
    columns = jnp.arange(length, dtype=jnp.int32)
    angles = angles_of(numbers[:, None], columns[None, :], length)
    return (jnp.cos(angles), jnp.sin(angles))


def split_table(table):
    table_high = table.astype(jnp.bfloat16)
    table_low = (table - table_high.astype(jnp.float32)).astype(jnp.bfloat16)
    return (table_high, table_low)


def member_grad(own, others, target, divisor):
    pulled = jnp.zeros_like(own)
    for other in others:
        pulled = pulled + (own - other) / distance(own, other)
    return (own - target) / distance(own, target) - pulled / divisor


def local(
    ensemble_starting_fields,
    observed,
    wave_of_slot,
    leg_forward,
    leg_inverse,
    spec_filter,
    gain_first,
    gain_second,
    weight_in,
    weight_out,
):
    lat_rows = ensemble_starting_fields.shape[1]
    length = ensemble_starting_fields.shape[2]
    channels = ensemble_starting_fields.shape[3]
    waves_all = wave_of_slot.shape[0]
    slots = leg_forward.shape[0]
    degrees = leg_forward.shape[1]
    parts = lax.axis_size("lat")
    members = lax.axis_size("member")
    if (
        lat_rows % 16 == 0
        and lat_rows % members == 0
        and slots % NUMBER == 0
        and slots >= 2 * NUMBER
        and lat_rows >= 2 * members
        and channels % LANES == 0
        and length % PART == 0
        and degrees % 16 == 0
        and slots * parts == waves_all
    ):
        return pipelined(
            ensemble_starting_fields[0],
            observed,
            wave_of_slot,
            leg_forward,
            leg_inverse,
            spec_filter,
            gain_first,
            gain_second,
            weight_in,
            weight_out,
        )
    values = ensemble_starting_fields[0].astype(jnp.float32)
    normed = layer_norm(values, gain_first).astype(jnp.bfloat16)
    cosines, sines = dft_tables(wave_of_slot, length)
    fwd_table = jnp.stack([cosines / length, -sines / length], 1).reshape(2 * waves_all, length)
    fwd_high, fwd_low = split_table(fwd_table)
    analysis = jnp.einsum("kj,ljc->klc", fwd_high, normed, preferred_element_type=jnp.float32)
    analysis = analysis + jnp.einsum(
        "kj,ljc->klc", fwd_low, normed, preferred_element_type=jnp.float32
    )
    analysis = analysis.astype(jnp.bfloat16).reshape(waves_all, 2, lat_rows, channels)
    spectra = lax.all_to_all(analysis, "lat", split_axis=0, concat_axis=2, tiled=True)
    local_waves = lax.dynamic_slice_in_dim(wave_of_slot, lax.axis_index("lat") * slots, slots)
    order = jnp.arange(degrees, dtype=jnp.int32)
    retain = (order[None, :] >= local_waves[:, None]).astype(jnp.float32)[:, None, :, None]
    filt_real = spec_filter[0]
    filt_imag = spec_filter[1]
    coeffs = (
        jnp.einsum("sln,srnc->srlc", leg_forward, spectra, preferred_element_type=jnp.float32)
        * retain
    )
    real_part = coeffs[:, 0]
    imag_part = coeffs[:, 1]
    filtered = jnp.stack(
        [
            real_part * filt_real - imag_part * filt_imag,
            real_part * filt_imag + imag_part * filt_real,
        ],
        1,
    ).astype(jnp.bfloat16)
    synthesis = jnp.einsum(
        "snl,srlc->srnc", leg_inverse, filtered, preferred_element_type=jnp.float32
    )
    synthesis = synthesis.astype(jnp.bfloat16)
    returned = lax.all_to_all(synthesis, "lat", split_axis=2, concat_axis=0, tiled=True)
    returned = returned.reshape(2 * waves_all, lat_rows, channels)
    weights_m = jnp.where(wave_of_slot == 0, 1.0, 2.0).astype(jnp.float32)[:, None]
    inv_table = jnp.stack([weights_m * cosines, -weights_m * sines], 1).reshape(
        2 * waves_all, length
    )
    inv_high, inv_low = split_table(inv_table)
    spectral_part = jnp.einsum("kj,klc->ljc", inv_high, returned, preferred_element_type=F32)
    spectral_part = spectral_part + jnp.einsum(
        "kj,klc->ljc", inv_low, returned, preferred_element_type=jnp.float32
    )
    harmonic_damped_field = values + spectral_part
    normed_two = (
        layer_norm(harmonic_damped_field, gain_second)
        .astype(jnp.bfloat16)
        .reshape(lat_rows * length, channels)
    )
    hidden = jax.nn.gelu(jnp.dot(normed_two, weight_in, preferred_element_type=jnp.float32)).astype(
        jnp.bfloat16
    )
    feedforward_result = jnp.dot(hidden, weight_out, preferred_element_type=jnp.float32).reshape(
        lat_rows, length, channels
    )
    predicted_field = (harmonic_damped_field + feedforward_result).astype(jnp.bfloat16)[None]
    gathered_fields = lax.all_to_all(
        predicted_field, "member", split_axis=2, concat_axis=0, tiled=True
    )
    block_cols = length // members
    first_col = lax.axis_index("member") * block_cols
    target = lax.dynamic_slice_in_dim(observed, first_col, block_cols, 1).astype(jnp.float32)
    others = [gathered_fields[member_index].astype(jnp.float32) for member_index in range(members)]
    grads = [
        member_grad(others[member_index], others, target, members - 1)
        for member_index in range(members)
    ]
    grads = jnp.stack(grads, 0).astype(jnp.bfloat16)
    proper_loss_slope = lax.all_to_all(grads, "member", split_axis=0, concat_axis=2, tiled=True)
    return (predicted_field, proper_loss_slope)


def solution(mesh):
    in_specs = (
        P("member", "lat", None, None),
        P("lat", None, None),
        P(),
        P("lat", None, None),
        P("lat", None, None),
        P(),
        P(),
        P(),
        P(),
        P(),
    )
    out_specs = (P("member", "lat", None, None), P("member", "lat", None, None))
    return jax.shard_map(local, mesh=mesh, in_specs=in_specs, out_specs=out_specs, check_vma=False)
```

```python
import functools
import math

import jax
import jax.numpy as jnp
from jax import lax
from jax.experimental import pallas as pl
from jax.experimental.pallas import tpu as pltpu
from jax.sharding import PartitionSpec as P


EPS_NORM = 1e-05
EPS_DIST = 1e-06
LANES = 128
BAND = 8
PART = 64
FINE = 16
SPAN = 256
EARLY = 1
HALVES = 1
LIMITS = (40,40,40,40)
NUMBER = 8
F32 = jnp.float32
BF16 = jnp.bfloat16


def layer_norm(values, scales):
    average = jnp.mean(values, -1, keepdims=True)
    centred = values - average
    spread = jnp.mean(centred * centred, -1, keepdims=True)
    return centred * lax.rsqrt(spread + EPS_NORM) * scales


def matmul(left, right):
    return jnp.dot(left, right, preferred_element_type=F32)


def params(mebibytes):
    return pltpu.CompilerParams(vmem_limit_bytes=mebibytes << 20)


def cost(flops, bytes_accessed):
    return pl.CostEstimate(flops=int(flops), bytes_accessed=int(bytes_accessed), transcendentals=0)


def anywhere():
    return pl.BlockSpec(memory_space=pl.ANY)


def analysis_body(parts, field_ref, gain_ref, table_ref, *refs):
    outs = refs[:parts]
    normed, held = refs[parts:]
    band, length, channels = field_ref.shape
    orders = table_ref.shape[0]
    each = orders // parts
    pair = normed.shape[0]

    def some_rows(step, carry):
        for lane in range(pair):
            row = step * pair + lane
            for start in range(0, length, PART):
                values = field_ref[row, start : start + PART, :].astype(F32)
                normed[lane, start : start + PART, :] = layer_norm(values, gain_ref[...]).astype(
                    BF16
                )
            lines = matmul(table_ref[...], normed[lane])
            for tile in range(channels // LANES):
                held[tile, pl.ds(pl.multiple_of(row * orders, orders), orders), :] = lines[
                    :, tile * LANES : (tile + 1) * LANES
                ]
        return carry

    lax.fori_loop(0, band // pair, some_rows, 0)
    for part in range(parts):

        def one_order(index, carry, part=part):
            for tile in range(channels // LANES):
                outs[part][index, :, tile * LANES : (tile + 1) * LANES] = held[
                    tile, pl.ds(part * each + index, band, stride=orders), :
                ].astype(BF16)
            return carry

        lax.fori_loop(0, each, one_order, 0, unroll=4)


def analyse(field, gain, table, parts, first, count):
    _, length, channels = field.shape
    orders = table.shape[0]
    each = orders // parts
    return pl.pallas_call(
        functools.partial(analysis_body, parts),
        grid=(count // BAND,),
        in_specs=[
            pl.BlockSpec((BAND, length, channels), lambda i: (first // BAND + i, 0, 0)),
            pl.BlockSpec((1, channels), lambda i: (0, 0)),
            pl.BlockSpec((orders, length), lambda i: (0, 0)),
        ],
        out_specs=[pl.BlockSpec((each, BAND, channels), lambda i: (0, i, 0))] * parts,
        out_shape=[jax.ShapeDtypeStruct((each, count, channels), BF16)] * parts,
        scratch_shapes=[
            pltpu.VMEM((4, length, channels), BF16),
            pltpu.VMEM((channels // LANES, BAND * orders, LANES), F32),
        ],
        compiler_params=params(LIMITS[0]),
        cost_estimate=cost(2 * count * orders * length * channels, 3 * count * length * channels),
    )(field, gain, table)


def spectral_body(parts, total, offsets, targets, passed, scalars, *refs):
    pieces = len(offsets)
    slabs = refs[: pieces * parts]
    forward_ref, inverse_ref, filter_ref = refs[pieces * parts : pieces * parts + 3]
    first = pieces * parts + 3 + passed
    count = len(targets) * parts
    outs = refs[first : first + count]
    spectra, held = refs[first + count :]
    slot = pl.program_id(0)
    own = scalars[0]
    wave = scalars[2 + slot]
    degrees, latitudes = forward_ref.shape[1:]
    channels = filter_ref.shape[2]
    for piece in range(pieces):
        for part in range(parts):
            slab = slabs[piece * parts + part]
            rows = slab.shape[1]
            origin = lax.bitwise_xor(own, part) * total + offsets[piece]
            place = pl.ds(pl.multiple_of(origin, rows), rows)
            for ri in range(2):
                spectra[ri, place, :] = slab[ri]
    order = lax.broadcasted_iota(jnp.int32, (degrees, 1), 0)
    retain = order >= wave
    for tile in range(channels // LANES):
        lanes = slice(tile * LANES, (tile + 1) * LANES)
        both = jnp.concatenate([spectra[0, :, lanes], spectra[1, :, lanes]], 1)
        coeffs = matmul(forward_ref[0], both)
        coeffs = jnp.where(retain, coeffs, 0.0)
        real_part, imag_part = coeffs[:, :LANES], coeffs[:, LANES:]
        filt_real, filt_imag = filter_ref[0, :, lanes], filter_ref[1, :, lanes]
        filtered = jnp.concatenate(
            [
                (real_part * filt_real - imag_part * filt_imag).astype(BF16),
                (real_part * filt_imag + imag_part * filt_real).astype(BF16),
            ],
            1,
        )
        profile = matmul(inverse_ref[0], filtered)
        for ri in range(2):
            start = pl.multiple_of((2 * slot + ri) * latitudes, latitudes)
            held[tile, pl.ds(start, latitudes), :] = profile[:, ri * LANES : (ri + 1) * LANES]

    @pl.when(slot == pl.num_programs(0) - 1)
    def _():
        for index, (offset, size) in enumerate(targets):
            for part in range(parts):
                out = outs[index * parts + part]
                base = lax.bitwise_xor(own, part) * total + offset

                def one_row(row, carry, out=out, base=base):
                    for tile in range(channels // LANES):
                        out[row, :, tile * LANES : (tile + 1) * LANES] = held[
                            tile, pl.ds(base + row, out.shape[1], stride=latitudes), :
                        ].astype(BF16)
                    return carry

                lax.fori_loop(0, size, one_row, 0, unroll=2)


def spectral(scalars, pieces, forward, inverse, spec_filter, first, number, targets):
    parts = len(pieces[0][1])
    degrees, latitudes = forward.shape[1:]
    channels = spec_filter.shape[2]
    operands = []
    in_specs = []
    for _, slabs in pieces:
        for slab in slabs:
            operands.append(slab)
            in_specs.append(pl.BlockSpec((2,) + slab.shape[1:], lambda s, *_: (s, 0, 0)))
    operands += [forward, inverse, spec_filter]
    in_specs += [
        pl.BlockSpec((1, degrees, latitudes), lambda s, *_: (first + s, 0, 0)),
        pl.BlockSpec((1, latitudes, degrees), lambda s, *_: (first + s, 0, 0)),
        pl.BlockSpec((2, degrees, channels), lambda s, *_: (0, 0, 0)),
    ]
    out_shape = []
    out_specs = []
    aliases = {}
    passed = 0
    for _, size, held_slots, block, carried in targets:
        for part in range(parts):
            if carried is not None:
                aliases[1 + len(operands)] = len(out_shape)
                operands.append(carried[part])
                in_specs.append(anywhere())
                passed += 1
            out_shape.append(jax.ShapeDtypeStruct((size, 2 * held_slots, channels), BF16))
            out_specs.append(
                pl.BlockSpec((size, 2 * number, channels), lambda s, *_, block=block: (0, block, 0))
            )
    outs = pl.pallas_call(
        functools.partial(
            spectral_body,
            parts,
            latitudes // parts,
            tuple(offset for offset, _ in pieces),
            tuple(target[:2] for target in targets),
            passed,
        ),
        grid_spec=pltpu.PrefetchScalarGridSpec(
            num_scalar_prefetch=1,
            grid=(number,),
            in_specs=in_specs,
            out_specs=out_specs,
            scratch_shapes=[
                pltpu.VMEM((2, latitudes, channels), BF16),
                pltpu.VMEM((channels // LANES, 2 * number * latitudes, LANES), F32),
            ],
        ),
        out_shape=out_shape,
        input_output_aliases=aliases,
        compiler_params=params(LIMITS[1]),
        cost_estimate=cost(
            8 * number * degrees * latitudes * channels,
            8 * number * latitudes * channels + 4 * number * degrees * latitudes,
        ),
    )(scalars, *operands)
    return [outs[index * parts : (index + 1) * parts] for index in range(len(targets))]


def finish_body(parts, members, continued, scalars, *refs):
    slabs = refs[:parts]
    field_ref, table_ref, gain_ref, into_ref, from_ref = refs[parts : parts + 5]
    first = parts + 5 + (1 if continued else 0)
    predicted_ref = refs[first]
    sends = refs[first + 1 : first + 1 + members]
    after_ref, normed_ref = refs[first + 1 + members :]
    length = field_ref.shape[1]
    lines = jnp.concatenate([slab[0] for slab in slabs], 0)
    after_ref[...] = matmul(table_ref[...], lines) + field_ref[0].astype(F32)
    for start in range(0, length, PART):
        normed_ref[start : start + PART, :] = layer_norm(
            after_ref[start : start + PART, :], gain_ref[...]
        ).astype(BF16)
    step = 256 if length % 256 == 0 else length
    for start in range(0, length, step):
        rows = slice(start, start + step)
        hidden = jax.nn.gelu(matmul(normed_ref[rows, :], into_ref[...])).astype(BF16)
        predicted_ref[0, rows, :] = (after_ref[rows, :] + matmul(hidden, from_ref[...])).astype(
            BF16
        )
    share = pl.num_programs(0) // members
    for part in range(members):

        @pl.when(pl.program_id(0) // share == part)
        def _(part=part):
            sends[part][0] = predicted_ref[0]


def finish(scalars, slabs, field, table, gain, into, out_of, carried, offset, members):
    parts = len(slabs)
    size, _, channels = slabs[0].shape
    _, length = field.shape[:2]
    share = size // members

    def position(r, sc):
        return lax.bitwise_xor(sc[1], r // share) * share + lax.rem(r, share)

    def whole(r, sc):
        return (offset + position(r, sc), 0, 0)

    def fixed(r, sc):
        return (0, 0)

    in_specs = [
        pl.BlockSpec((1,) + slab.shape[1:], lambda r, sc: (position(r, sc), 0, 0))
        for slab in slabs
    ]
    in_specs += [
        pl.BlockSpec((1, length, channels), whole),
        pl.BlockSpec(table.shape, fixed),
        pl.BlockSpec(gain.shape, fixed),
        pl.BlockSpec(into.shape, fixed),
        pl.BlockSpec(out_of.shape, fixed),
    ]
    aliases = {}
    if carried is not None:
        in_specs.append(anywhere())
        aliases = {1 + parts + 5: 0}
    out_specs = [pl.BlockSpec((1, length, channels), whole)]
    out_shape = [jax.ShapeDtypeStruct(field.shape, BF16)]
    for part in range(members):
        out_specs.append(
            pl.BlockSpec(
                (1, length, channels),
                lambda r, sc, part=part: (jnp.clip(r - part * share, 0, share - 1), 0, 0),
            )
        )
        out_shape.append(jax.ShapeDtypeStruct((share, length, channels), BF16))
    hidden = into.shape[1]
    return pl.pallas_call(
        functools.partial(finish_body, parts, members, carried is not None),
        grid_spec=pltpu.PrefetchScalarGridSpec(
            num_scalar_prefetch=1,
            grid=(size,),
            in_specs=in_specs,
            out_specs=out_specs,
            scratch_shapes=[
                pltpu.VMEM((length, channels), F32),
                pltpu.VMEM((length, channels), BF16),
            ],
        ),
        out_shape=out_shape,
        input_output_aliases=aliases,
        compiler_params=params(LIMITS[2]),
        cost_estimate=cost(
            2 * size * length * channels * (table.shape[1] + 2 * hidden),
            8 * size * length * channels,
        ),
    )(scalars, *slabs, field, table, gain, into, out_of, *([] if carried is None else [carried]))


def score_body(members, continued, scalars, *refs):
    fields = refs[:members]
    target_ref = refs[members]
    outs = refs[members + 1 + continued :]
    length, channels = target_ref.shape[1:]

    def one_part(index, carry):
        place = pl.ds(pl.multiple_of(index * FINE, FINE), FINE)
        values = [field[0, place, :].astype(F32) for field in fields]
        target = target_ref[0, place, :].astype(F32)

        def pull(first, second, scale):
            apart = first - second
            mean_square = jnp.sum(apart * apart, -1, keepdims=True) * (1.0 / channels)
            return apart * (lax.rsqrt(mean_square + EPS_DIST) * scale)

        slopes = [pull(value, target, 1.0) for value in values]
        for one in range(members):
            for other in range(one + 1, members):
                term = pull(values[one], values[other], 1.0 / (members - 1))
                slopes[one] = slopes[one] - term
                slopes[other] = slopes[other] + term
        for one in range(members):
            outs[one][0, place, :] = slopes[one].astype(BF16)
        return carry

    lax.fori_loop(0, length // FINE, one_part, 0, unroll=2)


def score(scalars, fields, observed, carried, offset):
    members = len(fields)
    share, length, channels = fields[0].shape

    def block(r, j, sc):
        return (r, j, 0)

    def whole(r, j, sc):
        return (offset + sc[1] * share + r, j, 0)

    span = SPAN if length % SPAN == 0 else length
    spec = pl.BlockSpec((1, span, channels), block)
    placed = pl.BlockSpec((1, span, channels), whole)
    piece = jax.ShapeDtypeStruct((share, length, channels), BF16)
    out_specs = [placed] + [spec] * (members - 1)
    out_shape = [jax.ShapeDtypeStruct(observed.shape, BF16)] + [piece] * (members - 1)
    continued = carried is not None
    return pl.pallas_call(
        functools.partial(score_body, members, continued),
        grid_spec=pltpu.PrefetchScalarGridSpec(
            num_scalar_prefetch=1,
            grid=(share, length // span),
            in_specs=[spec] * members + [placed] + [anywhere()] * continued,
            out_specs=out_specs,
        ),
        out_shape=out_shape,
        input_output_aliases={members + 2: 0} if continued else {},
        compiler_params=params(LIMITS[3]),
        cost_estimate=cost(100 * share * length * channels, 18 * share * length * channels),
    )(scalars, *fields, observed, *([carried] if continued else []))


def swap(array, axis, part):
    size = lax.axis_size(axis)
    return lax.ppermute(array, axis, [(i, i ^ part) for i in range(size)])


def exchange(slabs, axis):
    moved = [swap(slabs[part], axis, part) for part in range(len(slabs) - 1, 0, -1)]
    return [slabs[0]] + moved[::-1]


def place(whole, pieces):
    for piece, start in pieces:
        whole = lax.dynamic_update_slice_in_dim(whole, piece, start, 0)
    return whole


def angles_of(numbers, columns, length):
    phases = numbers * columns % length
    return phases.astype(F32) * (2.0 * math.pi / length)


def chunk_sizes(rows, unit):
    return (unit,) * (rows // unit)


def pipelined(
    field,
    observed,
    wave_of_slot,
    leg_forward,
    leg_inverse,
    spec_filter,
    gain_first,
    gain_second,
    weight_in,
    weight_out,
):
    rows, length, channels = field.shape
    slots = leg_forward.shape[0]
    parts = lax.axis_size("lat")
    members = lax.axis_size("member")
    own = lax.axis_index("lat")
    own_member = lax.axis_index("member")
    number = NUMBER
    groups = slots // number
    chunks = chunk_sizes(rows, members)
    gain_first = gain_first.reshape(1, channels)
    gain_second = gain_second.reshape(1, channels)
    scalars = jnp.stack([own, own_member]).astype(jnp.int32)

    waves = wave_of_slot.reshape(parts, groups, number)
    steps = jnp.arange(parts, dtype=jnp.int32)
    columns = jnp.arange(length, dtype=jnp.int32)
    waves = jnp.take(waves, own ^ steps, axis=0)
    turn = (jnp.arange(2, dtype=jnp.int32) == 0)[:, None]

    def outgoing(group):
        angles = angles_of(waves[:, group, :, None, None], columns, length)
        table = jnp.where(turn, jnp.cos(angles), -jnp.sin(angles)) * (1.0 / length)
        return table.astype(BF16).reshape(parts * number * 2, length)

    tables = [outgoing(group) for group in range(groups)]
    incoming = jnp.repeat(waves.reshape(-1), 2)
    angles = angles_of(incoming[None, :], columns[:, None], length)
    weights = jnp.where(incoming == 0, 1.0, 2.0).astype(F32)[None, :]
    even = (jnp.arange(incoming.shape[0]) % 2 == 0)[None, :]
    back_table = (weights * jnp.where(even, jnp.cos(angles), -jnp.sin(angles))).astype(BF16)
    local_waves = lax.dynamic_slice_in_dim(wave_of_slot, own * slots, slots)

    received = []
    for group in range(groups):
        halves = HALVES if group == 0 else 1
        pieces = []
        for half in range(halves):
            count = rows // halves
            slabs = analyse(field, gain_first, tables[group], parts, half * count, count)
            pieces.append((half * count, exchange(slabs, "lat")))
        received.append(pieces)
    starts = [sum(chunks[:index]) for index in range(len(chunks))]
    early = [None] * EARLY
    profiles = [None] * len(chunks)
    for group in range(groups):
        numbers = jnp.concatenate(
            [scalars, local_waves[group * number : (group + 1) * number]]
        )
        last = group == groups - 1
        targets = []
        for index in range(len(chunks)):
            place_of = (starts[index], chunks[index])
            if index >= EARLY:
                targets.append(place_of + (slots, group, profiles[index]))
            elif last:
                targets.append(place_of + (number, 0, None))
            else:
                targets.append(place_of + (slots - number, group, early[index]))
        profiles = spectral(
            numbers,
            received[group],
            leg_forward,
            leg_inverse,
            spec_filter,
            group * number,
            number,
            targets,
        )
        if not last:
            early = profiles[:EARLY]
        if group == groups - 2:
            arrived = []
            for index in range(EARLY):
                arrived.append(exchange(early[index], "lat"))

    predicted = None
    slope = None
    offset = 0
    placed = []
    for index, size in enumerate(chunks):
        slabs = exchange(profiles[index], "lat")
        if index < EARLY:
            slabs = [slab for both in zip(arrived[index], slabs) for slab in both]
        predicted, *sends = finish(
            scalars,
            slabs,
            field,
            back_table,
            gain_second,
            weight_in,
            weight_out,
            predicted,
            offset,
            members,
        )
        fields = exchange(sends, "member")
        slope, *grads = score(scalars, fields, observed, slope, offset)
        share = size // members
        back = exchange([None] + grads, "member")
        pieces = [
            (back[part], offset + (own_member ^ part) * share) for part in range(1, members)
        ]
        placed.append(pieces)
        offset += size
        if index >= 2:
            slope = place(slope, placed[index - 2])
    for pieces in placed[max(len(chunks) - 2, 0) :]:
        slope = place(slope, pieces)
    return predicted[None], slope[None]


def distance(first, second):
    return jnp.sqrt(jnp.mean(jnp.square(first - second), -1, keepdims=True) + EPS_DIST)


def dft_tables(numbers, length):
    columns = jnp.arange(length, dtype=jnp.int32)
    angles = angles_of(numbers[:, None], columns[None, :], length)
    return (jnp.cos(angles), jnp.sin(angles))


def split_table(table):
    table_high = table.astype(jnp.bfloat16)
    table_low = (table - table_high.astype(jnp.float32)).astype(jnp.bfloat16)
    return (table_high, table_low)


def member_grad(own, others, target, divisor):
    pulled = jnp.zeros_like(own)
    for other in others:
        pulled = pulled + (own - other) / distance(own, other)
    return (own - target) / distance(own, target) - pulled / divisor


def local(
    ensemble_starting_fields,
    observed,
    wave_of_slot,
    leg_forward,
    leg_inverse,
    spec_filter,
    gain_first,
    gain_second,
    weight_in,
    weight_out,
):
    lat_rows = ensemble_starting_fields.shape[1]
    length = ensemble_starting_fields.shape[2]
    channels = ensemble_starting_fields.shape[3]
    waves_all = wave_of_slot.shape[0]
    slots = leg_forward.shape[0]
    degrees = leg_forward.shape[1]
    parts = lax.axis_size("lat")
    members = lax.axis_size("member")
    if (
        lat_rows % 16 == 0
        and lat_rows % members == 0
        and parts & (parts - 1) == 0
        and members & (members - 1) == 0
        and slots % NUMBER == 0
        and slots >= 2 * NUMBER
        and lat_rows >= 2 * members
        and channels % LANES == 0
        and length % PART == 0
        and degrees % 16 == 0
        and slots * parts == waves_all
    ):
        return pipelined(
            ensemble_starting_fields[0],
            observed,
            wave_of_slot,
            leg_forward,
            leg_inverse,
            spec_filter,
            gain_first,
            gain_second,
            weight_in,
            weight_out,
        )
    values = ensemble_starting_fields[0].astype(jnp.float32)
    normed = layer_norm(values, gain_first).astype(jnp.bfloat16)
    cosines, sines = dft_tables(wave_of_slot, length)
    fwd_table = jnp.stack([cosines / length, -sines / length], 1).reshape(2 * waves_all, length)
    fwd_high, fwd_low = split_table(fwd_table)
    analysis = jnp.einsum("kj,ljc->klc", fwd_high, normed, preferred_element_type=jnp.float32)
    analysis = analysis + jnp.einsum(
        "kj,ljc->klc", fwd_low, normed, preferred_element_type=jnp.float32
    )
    analysis = analysis.astype(jnp.bfloat16).reshape(waves_all, 2, lat_rows, channels)
    spectra = lax.all_to_all(analysis, "lat", split_axis=0, concat_axis=2, tiled=True)
    local_waves = lax.dynamic_slice_in_dim(wave_of_slot, lax.axis_index("lat") * slots, slots)
    order = jnp.arange(degrees, dtype=jnp.int32)
    retain = (order[None, :] >= local_waves[:, None]).astype(jnp.float32)[:, None, :, None]
    filt_real = spec_filter[0]
    filt_imag = spec_filter[1]
    coeffs = (
        jnp.einsum("sln,srnc->srlc", leg_forward, spectra, preferred_element_type=jnp.float32)
        * retain
    )
    real_part = coeffs[:, 0]
    imag_part = coeffs[:, 1]
    filtered = jnp.stack(
        [
            real_part * filt_real - imag_part * filt_imag,
            real_part * filt_imag + imag_part * filt_real,
        ],
        1,
    ).astype(jnp.bfloat16)
    synthesis = jnp.einsum(
        "snl,srlc->srnc", leg_inverse, filtered, preferred_element_type=jnp.float32
    )
    synthesis = synthesis.astype(jnp.bfloat16)
    returned = lax.all_to_all(synthesis, "lat", split_axis=2, concat_axis=0, tiled=True)
    returned = returned.reshape(2 * waves_all, lat_rows, channels)
    weights_m = jnp.where(wave_of_slot == 0, 1.0, 2.0).astype(jnp.float32)[:, None]
    inv_table = jnp.stack([weights_m * cosines, -weights_m * sines], 1).reshape(
        2 * waves_all, length
    )
    inv_high, inv_low = split_table(inv_table)
    spectral_part = jnp.einsum("kj,klc->ljc", inv_high, returned, preferred_element_type=F32)
    spectral_part = spectral_part + jnp.einsum(
        "kj,klc->ljc", inv_low, returned, preferred_element_type=jnp.float32
    )
    harmonic_damped_field = values + spectral_part
    normed_two = (
        layer_norm(harmonic_damped_field, gain_second)
        .astype(jnp.bfloat16)
        .reshape(lat_rows * length, channels)
    )
    hidden = jax.nn.gelu(jnp.dot(normed_two, weight_in, preferred_element_type=jnp.float32)).astype(
        jnp.bfloat16
    )
    feedforward_result = jnp.dot(hidden, weight_out, preferred_element_type=jnp.float32).reshape(
        lat_rows, length, channels
    )
    predicted_field = (harmonic_damped_field + feedforward_result).astype(jnp.bfloat16)[None]
    gathered_fields = lax.all_to_all(
        predicted_field, "member", split_axis=2, concat_axis=0, tiled=True
    )
    block_cols = length // members
    first_col = lax.axis_index("member") * block_cols
    target = lax.dynamic_slice_in_dim(observed, first_col, block_cols, 1).astype(jnp.float32)
    others = [gathered_fields[member_index].astype(jnp.float32) for member_index in range(members)]
    grads = [
        member_grad(others[member_index], others, target, members - 1)
        for member_index in range(members)
    ]
    grads = jnp.stack(grads, 0).astype(jnp.bfloat16)
    proper_loss_slope = lax.all_to_all(grads, "member", split_axis=0, concat_axis=2, tiled=True)
    return (predicted_field, proper_loss_slope)


def solution(mesh):
    in_specs = (
        P("member", "lat", None, None),
        P("lat", None, None),
        P(),
        P("lat", None, None),
        P("lat", None, None),
        P(),
        P(),
        P(),
        P(),
        P(),
    )
    out_specs = (P("member", "lat", None, None), P("member", "lat", None, None))
    return jax.shard_map(local, mesh=mesh, in_specs=in_specs, out_specs=out_specs, check_vma=False)
```
